32 devices in a mesh: parts: 2 (over y), users: 16 (over z, x, core).
Axes of the slice: x: 2, y: 2, z: 4, core: 2. Of those that a mesh axis runs over, the one named last changes fastest.
Arguments:
- candidates: bfloat16 [512, 512], P(('parts', 'users')), parts along dimension 0, may hold values from -6 to 6
- candidate_user: int32 [512], P(('parts', 'users')), parts along dimension 0, may hold values from 0 to 7
- events: bfloat16 [65536, 512], P(('parts', 'users')), parts along dimension 0, may hold values from -6 to 6
- event_user: int32 [65536], P(('parts', 'users')), parts along dimension 0, may hold values from 0 to 7, never falling along the last dimension, each value on 1 to 12288 neighbouring positions
- event_mask: int32 [65536], P(('parts', 'users')), parts along dimension 0, may hold values 0 or 1
- query_weight: bfloat16 [512, 512], replicated, may hold values from -0.25 to 0.25
- key_weight: bfloat16 [512, 512], replicated, may hold values from -0.25 to 0.25
- value_weight: bfloat16 [512, 512], replicated, may hold values from -2 to 2
- gate_weight: bfloat16 [512, 512], replicated, may hold values from -0.25 to 0.25
- output_weight: bfloat16 [512, 512], replicated, may hold values from -0.25 to 0.25
Outputs:
- candidate_out: bfloat16 [512, 512], P(('parts', 'users')), parts along dimension 0
The draws below stay inside these ranges and needn't reach their ends.
There are 2 independent parts, one for each index of `parts`. The reference program is written for one: setup_inputs(seed, part) draws one part's arguments, and reference() takes and returns one part's arrays. A program takes and returns all parts, laid end to end along the dimension named above; an argument that names none is the same for every part. Nothing has to cross between parts.
Inputs may be any that keep to these rules, and one draw needn't show every extreme that they name: event_user never falls along the events; each user's events form one run of at most 12288 slots.
All inputs are finite; a program needn't handle non-finite values. No bound on the sum of `event_mask` on one device may be relied on, other than what follows from the above.
Results may differ from the reference program's by a relative error of at most 0.0044.
Values may be sent and summed in bfloat16 or wider, within the bound.
No kernel may reach another device: no remote copies, remote signals or barrier semaphores. Data moves between devices by JAX's collectives and lax.ppermute only.
A program may use at most 64 MiB of HBM per device.

```python
import math
import jax
import jax.numpy as jnp
import numpy as np
from jax import lax

D = 512
HEADS = 4
DH = 128
USERS = 8
EV_DEV = 2048
CANDS = 256
EVENTS = 32768
MOST = 12288
N_USERS = 16


def draw_value_weight(key, part):
    normal_key, scale_key = jax.random.split(key, 2)
    entries = jnp.clip(jax.random.normal(normal_key, (D, D), jnp.float32), -6.0, 6.0)
    column_scale = jnp.exp(jax.random.uniform(scale_key, (1, D), jnp.float32, jnp.log(0.3), jnp.log(3.0)))
    return (entries * column_scale / jnp.sqrt(D * 1.0)).astype(jnp.bfloat16)


def set_ends(values, own_key, smallest, high):
    place = [jax.random.randint(jax.random.fold_in(own_key, axis), (), 0, length) for axis, length in enumerate(values.shape)]
    longest = values.shape.index(max(values.shape))
    neighbour = place[:longest] + [(place[longest] + 1) % values.shape[longest]] + place[longest + 1:]
    return values.at[tuple(place)].set(smallest).at[tuple(neighbour)].set(high)


def block_levels(key, extent, cuts, smallest, top_value):
    level = 1.0
    for dim, blocks in cuts:
        steps = jax.random.uniform(jax.random.fold_in(jax.random.fold_in(key, 6), dim), (blocks,), jnp.float32, smallest / len(cuts), top_value / len(cuts))
        level = level * jnp.repeat(jnp.exp(steps), extent[dim] // blocks).reshape((-1,) + (1,) * (len(extent) - 1 - dim))
    return level


def length_profile(count, total, limit, skew):
    loads = [(1 << 20) // math.isqrt(standing ** skew) + 1 for standing in range(2, count + 1)]
    surplus, holding = total - limit - (count - 1), [1] * (count - 1)
    while surplus > 0:
        free = [i for i in range(count - 1) if holding[i] < limit]
        whole, remaining = sum([loads[i] for i in free]), surplus
        for i in free:
            more = min(limit - holding[i], max(1, remaining * loads[i] // whole), surplus)
            holding[i] = holding[i] + more
            surplus = surplus - more
    return np.array([limit] + holding)


def uneven_parts(rng, amount, total, limit, skew):
    if amount == 2:
        one = jax.random.randint(rng, (), max(1, total - limit), min(limit, total - 1) + 1)
        return jnp.stack([one, total - one])
    tallies = jnp.asarray(length_profile(amount, total, limit, skew), jnp.int32)
    couples = (amount - 1) // 2
    giver, taker = tallies[1:1 + 2 * couples:2], tallies[2:2 + 2 * couples:2]
    slack = jnp.minimum(giver - 1, limit - taker)
    passed = jax.random.randint(jax.random.fold_in(rng, 1), (couples,), 0, 1 << 20) % (slack + 1)
    tallies = tallies.at[1:1 + 2 * couples:2].set(giver - passed).at[2:2 + 2 * couples:2].set(taker + passed)
    return tallies[jax.random.permutation(jax.random.fold_in(rng, 2), amount)]


def noise(own_key, extent, scale, reach, pieces=(), dtype=jnp.bfloat16):
    level = block_levels(own_key, extent, pieces, -0.22, 0.18) if pieces else 1.0
    array = jax.random.normal(own_key, extent, jnp.float32) * scale * level
    return jnp.minimum(jnp.maximum(array, -reach), reach).astype(dtype)


def setup_inputs(seed: int = 0, part: int = 0) -> dict:
    keys = jax.random.split(jax.random.key(seed), 11)
    own_keys = jax.random.split(jax.random.fold_in(keys[10], part), 11)
    return {
        "candidates": noise(own_keys[0], (CANDS, D), 1.0, 6.0, ((0, 16),)),
        "candidate_user": set_ends(jax.random.randint(own_keys[1], (CANDS,), 0, USERS), jax.random.fold_in(own_keys[1], 1), 0, USERS - 1).astype(jnp.int32),
        "events": noise(own_keys[2], (EVENTS, D), 1.0, 6.0, ((0, 16),)),
        "event_user": jnp.searchsorted(jnp.cumsum(uneven_parts(own_keys[3], USERS, EVENTS, MOST, 2)), jnp.arange(EVENTS), side="right").astype(jnp.int32),
        "event_mask": set_ends((jax.random.randint(own_keys[4], (EVENTS,), 0, 4) < 3).astype(jnp.int32), jax.random.fold_in(own_keys[4], 1), 0, 1),
        "query_weight": noise(keys[5], (D, D), D ** -0.5, 0.25),
        "key_weight": noise(keys[6], (D, D), D ** -0.5, 0.25),
        "value_weight": draw_value_weight(jax.random.fold_in(keys[10], 71), part),
        "gate_weight": noise(keys[8], (D, D), D ** -0.5, 0.25),
        "output_weight": noise(keys[9], (D, D), D ** -0.5, 0.25),
    }


def reference(candidates, candidate_user, events, event_user, event_mask, query_weight, key_weight, value_weight, gate_weight, output_weight):
    queries = jnp.dot(candidates, query_weight, preferred_element_type=jnp.float32).astype(jnp.bfloat16)
    gate_values = jax.nn.silu(jnp.dot(candidates, gate_weight, preferred_element_type=jnp.float32))
    key_rows = jnp.dot(events, key_weight, preferred_element_type=jnp.float32).astype(jnp.bfloat16)
    value_rows = jnp.dot(events, value_weight, preferred_element_type=jnp.float32).astype(jnp.bfloat16)
    score_scale = 1.0 / math.sqrt(DH)
    query_heads = queries.astype(jnp.float32).reshape(CANDS, HEADS, DH)
    key_blocks = key_rows.astype(jnp.float32).reshape(N_USERS, EV_DEV, HEADS, DH)
    value_blocks = value_rows.astype(jnp.float32).reshape(N_USERS, EV_DEV, HEADS, DH)
    user_blocks = event_user.reshape(N_USERS, EV_DEV)
    mask_blocks = event_mask.astype(jnp.float32).reshape(N_USERS, EV_DEV)

    def add_block(summed, block_items):
        key_part, value_part, user_part, mask_part = block_items
        scores = jnp.einsum('chd,ehd->hce', query_heads, key_part) * score_scale
        same_user = (candidate_user[:, None] == user_part[None, :]).astype(jnp.float32) * mask_part[None, :]
        attn_weights = (jax.nn.silu(scores) * same_user[None]).astype(jnp.bfloat16).astype(jnp.float32)
        return (summed + jnp.einsum('hce,ehd->chd', attn_weights, value_part).reshape(CANDS, D), None)
    summed, _ = lax.scan(add_block, jnp.zeros((CANDS, D), jnp.float32), (key_blocks, value_blocks, user_blocks, mask_blocks))
    mean_row = lax.optimization_barrier(jnp.mean(summed, axis=1, keepdims=True))
    centred = summed - mean_row
    var_row = lax.optimization_barrier(jnp.mean(centred * centred, axis=1, keepdims=True))
    normed = centred / jnp.sqrt(var_row + 1e-05)
    gated_rows = (normed * gate_values).astype(jnp.bfloat16)
    result = candidates.astype(jnp.float32) + jnp.dot(gated_rows, output_weight, preferred_element_type=jnp.float32)
    return result.astype(jnp.bfloat16)
```

```python
import functools
import math

import jax
import jax.numpy as jnp
from jax import lax
from jax.experimental import pallas as pl
from jax.experimental.pallas import tpu as pltpu
from jax.sharding import PartitionSpec as P

HEADS = 4
LANES = 128
WINDOW = 64
TILE = 512
AXIS = "users"


def reverse_bits(value, count):
    out = 0
    for bit in range(count):
        out |= ((value >> bit) & 1) << (count - 1 - bit)
    return out


def attention_kernel(
    bounds_ref,
    me_ref,
    gathered_ref,
    query_weight_ref,
    masked_user_ref,
    *refs,
    chunks,
    tile,
    own_count,
    group_count,
    scale,
):
    key_refs = refs[:chunks]
    value_refs = refs[chunks : 2 * chunks]
    out_ref, perm_ref, even_ref, odd_ref, owner_ref, total_ref = refs[2 * chunks :]
    rows, wide = gathered_ref.shape
    width = query_weight_ref.shape[0]
    block = min(rows, 256)
    blocks = rows // block

    def for_blocks(body):
        if blocks == 1:
            body(0)
        else:
            pl.loop(0, blocks)(body)

    def block_start(index):
        return pl.multiple_of(index * block, block) if blocks > 1 else 0

    owner = gathered_ref[:, width:wide].astype(jnp.float32)
    order = lax.broadcasted_iota(jnp.int32, owner.shape, 0).astype(jnp.float32)
    sort_key = owner * float(rows) + order
    key_row = jnp.transpose(sort_key)[0:1, :]
    owner_row = jnp.transpose(owner)[0:1, :]
    owner_ref[pl.ds(0, rows), :] = sort_key

    def add_rank(index, rank):
        piece = owner_ref[pl.ds(block_start(index), block), :]
        piece = jnp.concatenate([piece] * (rows // LANES), axis=1)
        return rank + jnp.sum(jnp.where(piece < key_row, 1.0, 0.0), axis=0, keepdims=True)

    rank = jnp.zeros((1, rows), jnp.float32)
    if blocks == 1:
        rank = add_rank(0, rank)
    else:
        rank = lax.fori_loop(0, blocks, add_rank, rank)
    rank = rank.astype(jnp.int32)

    owner_ref[pl.ds(rows, WINDOW), :] = jnp.full((WINDOW, LANES), -2.0, jnp.float32)
    even_ref[pl.ds(rows, WINDOW), :] = jnp.zeros((WINDOW, width), jnp.bfloat16)
    odd_ref[pl.ds(rows, WINDOW), :] = jnp.zeros((WINDOW, width), jnp.bfloat16)

    def sort_rows(index):
        start = block_start(index)
        place = lax.broadcasted_iota(jnp.int32, (block, rows), 0) + start
        chosen = jnp.where(place == rank, 1.0, 0.0).astype(jnp.bfloat16)
        perm_ref[pl.ds(start, block), :] = chosen
        ordered = jnp.dot(chosen, gathered_ref[...], preferred_element_type=jnp.float32)
        owner_ref[pl.ds(start, block), :] = ordered[:, width:wide]
        queries = jnp.dot(
            ordered[:, :width].astype(jnp.bfloat16),
            query_weight_ref[...],
            preferred_element_type=jnp.float32,
        ).astype(jnp.bfloat16)
        head = lax.broadcasted_iota(jnp.int32, queries.shape, 1) // (width // HEADS)
        is_even = head % 2 == 0
        zero = jnp.zeros_like(queries)
        even_ref[pl.ds(start, block), :] = jnp.where(is_even, queries, zero)
        odd_ref[pl.ds(start, block), :] = jnp.where(is_even, zero, queries)

    for_blocks(sort_rows)
    total_ref[...] = jnp.zeros_like(total_ref)

    head_size = width // HEADS
    pair = 2 * head_size
    chunk_rows = key_refs[0].shape[0]
    tiles_per_chunk = chunk_rows // tile
    for t in range(chunks * tiles_per_chunk):
        chunk, part = divmod(t, tiles_per_chunk)
        rows_of = pl.ds(part * tile, tile)
        low = bounds_ref[t, 0].astype(jnp.float32)
        high = bounds_ref[t, 1].astype(jnp.float32)
        first = jnp.sum(jnp.where(owner_row < low, 1.0, 0.0)).astype(jnp.int32)
        last = jnp.sum(jnp.where(owner_row <= high, 1.0, 0.0)).astype(jnp.int32)
        first = (first // 16) * 16
        windows = (last - first + WINDOW - 1) // WINDOW

        @pl.loop(0, windows)
        def _(w, chunk=chunk, rows_of=rows_of, first=first, t=t):
            at = pl.ds(pl.multiple_of(first + w * WINDOW, 16), WINDOW)
            mine = owner_ref[at, :]
            mine = jnp.concatenate([mine] * (tile // LANES), axis=1)
            same = mine == masked_user_ref[pl.ds(t, 1), :]
            same = jnp.concatenate([same, same], axis=0)
            for p in range(HEADS // 2):
                columns = pl.ds(p * pair, pair)
                lhs = jnp.concatenate([even_ref[at, columns], odd_ref[at, columns]], axis=0)
                half = lax.dot_general(
                    lhs,
                    key_refs[chunk][rows_of, columns],
                    (((1,), (1,)), ((), ())),
                    preferred_element_type=jnp.float32,
                ) * (0.5 * scale)
                attn = jnp.where(same, half + half * jnp.tanh(half), 0.0).astype(jnp.bfloat16)
                mixed = jnp.dot(
                    attn, value_refs[chunk][rows_of, columns], preferred_element_type=jnp.float32
                )
                total_ref[at, pl.ds(p * pair, head_size)] += mixed[:WINDOW, :head_size]
                total_ref[at, pl.ds(p * pair + head_size, head_size)] += mixed[WINDOW:, head_size:]

    me = me_ref[0]
    half_group = group_count // 2
    bits = half_group.bit_length() - 1

    def put_back(index):
        start = block_start(index)
        back = lax.dot_general(
            perm_ref[:, pl.ds(start, block)],
            total_ref[pl.ds(0, rows), :].astype(jnp.bfloat16),
            (((0,), (0,)), ((), ())),
            preferred_element_type=jnp.float32,
        ).astype(jnp.bfloat16)
        for k in range(block // own_count):
            if blocks == 1:
                p = k
                side, reverse = (p // half_group) * half_group, reverse_bits(p % half_group, bits)
            else:
                p = index * (block // own_count) + k
                side = (p // half_group) * half_group
                low_bits = p % half_group
                reverse = 0
                for b in range(bits):
                    reverse = reverse | (((low_bits >> b) & 1) << (bits - 1 - b))
            target = side + (lax.shift_right_logical(me, 1) ^ reverse)
            out_ref[pl.ds(pl.multiple_of(target * own_count, own_count), own_count), :] = back[
                k * own_count : (k + 1) * own_count, :
            ]

    for_blocks(put_back)


def per_device(
    group_count,
    candidates,
    candidate_user,
    events,
    event_user,
    event_mask,
    query_weight,
    key_weight,
    value_weight,
    gate_weight,
    output_weight,
):
    own_count, width = candidates.shape
    event_count = events.shape[0]
    me = lax.axis_index(AXIS)
    tagged = jnp.concatenate(
        [
            candidates,
            jnp.broadcast_to(candidate_user.astype(jnp.bfloat16)[:, None], (own_count, LANES)),
        ],
        axis=1,
    )
    gathered = tagged
    step = group_count // 2
    while step >= 1:
        other = lax.ppermute(gathered, AXIS, [(i, i ^ step) for i in range(group_count)])
        gathered = jnp.concatenate([gathered, other], axis=0)
        step //= 2

    chunks = 2
    chunk_rows = event_count // chunks
    keys, values = [], []
    for c in range(chunks):
        piece = events[c * chunk_rows : (c + 1) * chunk_rows]
        keys.append(
            jnp.dot(piece, key_weight, preferred_element_type=jnp.float32).astype(jnp.bfloat16)
        )
        values.append(
            jnp.dot(piece, value_weight, preferred_element_type=jnp.float32).astype(jnp.bfloat16)
        )
    gate_values = jax.nn.silu(jnp.dot(candidates, gate_weight, preferred_element_type=jnp.float32))
    tiles = event_count // TILE
    by_tile = event_user.reshape(tiles, TILE)
    bounds = jnp.concatenate([by_tile[:, :1], by_tile[:, TILE - 1 :]], axis=1)
    masked_user = jnp.where(event_mask.reshape(tiles, TILE) == 1, by_tile, -1).astype(jnp.float32)

    rows = gathered.shape[0]
    vmem = pl.BlockSpec(memory_space=pltpu.VMEM)
    smem = pl.BlockSpec(memory_space=pltpu.SMEM)
    partial_sums = pl.pallas_call(
        functools.partial(
            attention_kernel,
            chunks=chunks,
            tile=TILE,
            own_count=own_count,
            group_count=group_count,
            scale=1.0 / math.sqrt(width // HEADS),
        ),
        out_shape=jax.ShapeDtypeStruct((rows, width), jnp.bfloat16),
        in_specs=[smem, smem] + [vmem] * (3 + 2 * chunks),
        out_specs=vmem,
        scratch_shapes=[
            pltpu.VMEM((rows, rows), jnp.bfloat16),
            pltpu.VMEM((rows + WINDOW, width), jnp.bfloat16),
            pltpu.VMEM((rows + WINDOW, width), jnp.bfloat16),
            pltpu.VMEM((rows + WINDOW, LANES), jnp.float32),
            pltpu.VMEM((rows + WINDOW, width), jnp.float32),
        ],
        name="attention",
    )(bounds, me.reshape(1), gathered, query_weight, masked_user, *keys, *values)

    half_rows = rows // 2
    from_pair = lax.ppermute(
        partial_sums[half_rows:], AXIS, [(i, i ^ 1) for i in range(group_count)]
    )
    chip_sums = (
        partial_sums[:half_rows].astype(jnp.float32) + from_pair.astype(jnp.float32)
    ).astype(jnp.bfloat16)
    groups = [[core + 2 * i for i in range(group_count // 2)] for core in range(2)]
    spread = lax.all_to_all(
        chip_sums.reshape(group_count // 2, own_count, width),
        AXIS,
        0,
        0,
        axis_index_groups=groups,
    )
    summed = jnp.sum(spread.astype(jnp.float32), axis=0)
    mean_row = jnp.mean(summed, axis=1, keepdims=True)
    centred = summed - mean_row
    var_row = jnp.mean(centred * centred, axis=1, keepdims=True)
    normed = centred / jnp.sqrt(var_row + 1e-05)
    gated_rows = (normed * gate_values).astype(jnp.bfloat16)
    result = candidates.astype(jnp.float32) + jnp.dot(
        gated_rows, output_weight, preferred_element_type=jnp.float32
    )
    return result.astype(jnp.bfloat16)


def solution(mesh):
    spread = P(("parts", AXIS), None)
    flat = P(("parts", AXIS))
    in_specs = (spread, flat, spread, flat, flat, P(), P(), P(), P(), P())
    return jax.shard_map(
        functools.partial(per_device, mesh.shape[AXIS]),
        mesh=mesh,
        in_specs=in_specs,
        out_specs=spread,
        check_vma=False,
    )
```
